32 devices in a mesh: gx: 8 (over z, y), gy: 4 (over x, core).
Axes of the slice: x: 2, y: 2, z: 4, core: 2. Of those that a mesh axis runs over, the one named last changes fastest.
Arguments:
- fluid_vel: float32 [3, 64, 64, 256], P(None, 'gx', 'gy'), may hold values from -6 to 6
- part_pos: float32 [8192, 3, 128], P(('gx', 'gy')), may hold values from 0 to 1
- part_vel: float32 [8192, 3, 128], P(('gx', 'gy')), may hold values from -6 to 6
- brick_owner: int32 [8192, 1], P(('gx', 'gy')), may hold values from 0 to 31; in each aligned block of 256 rows (0 to 255, 256 to 511, ...) at most 16 rows name the same one
- brick_local: int32 [8192], P(('gx', 'gy')), may hold values from 0 to 255
- cell_in_brick: int32 [8192, 128], P(('gx', 'gy')), may hold values from 0 to 127
- pair_self: int32 [2, 16384], P(None, ('gx', 'gy')), may hold values from 0 to 255
- pair_other: int32 [2, 16384], P(None, ('gx', 'gy')), may hold values from 0 to 287
- halo_list: int32 [1024], P(('gx', 'gy')), may hold values from 0 to 255
Outputs:
- fluid_new: float32 [3, 64, 64, 256], P(None, 'gx', 'gy')
- pos_out: float32 [8192, 3, 128], P(('gx', 'gy'))
- vel_out: float32 [8192, 3, 128], P(('gx', 'gy'))
The draws below stay inside these ranges and needn't reach their ends.
Inputs may be any that keep to these rules, and one draw needn't show every extreme that they name: `brick_owner`: within the 256 blocks of one device (aligned blocks of rows), no tile is named more than 16 times, a bound that some block reaches.
All inputs are finite; a program needn't handle non-finite values.
Results may differ from the reference program's by a relative error of at most 0.0001.
Values sent between devices are 32-bit elements; how exact they have to be, the bound alone decides.
A program may use at most 64 MiB of HBM per device.

```python
import math
import jax
import jax.numpy as jnp
import numpy as np
from jax import lax

CX = 8
CY = 16
NZ = 256
BLK_DEV = 256
PAIRS_DEV = 512
HB = 16
SUBSTEPS = 2
PER_BLOCK = 128
BRICK_X = 2
BRICK_Y = 4
BRICK_Z = 16
NX = 64
NY = 64
TILES = 32
BRICKS_DEV = 256
BLOCKS = 8192
PAIRS = 16384
HALO_ROWS = 1024
CAP = 16
N_GX = 8
N_GY = 4


def set_ends(values, key, smallest, high):
    spot = [jax.random.randint(jax.random.fold_in(key, axis), (), 0, length) for axis, length in enumerate(values.shape)]
    longest = values.shape.index(max(values.shape))
    next_to = spot[:longest] + [(spot[longest] + 1) % values.shape[longest]] + spot[longest + 1:]
    return values.at[tuple(spot)].set(smallest).at[tuple(next_to)].set(high)


def levels(stream_key, shape, shards, low, top_value):
    loudness, own = 1.0, jax.random.fold_in(stream_key, 6)
    for dim, shards_of in shards:
        draws = jnp.exp(jax.random.uniform(jax.random.fold_in(own, dim), (shards_of,), jnp.float32, low / len(shards), top_value / len(shards)))
        loudness = loudness * jnp.repeat(draws, shape[dim] // shards_of).reshape([-1 if axis == dim else 1 for axis in range(len(shape))])
    return loudness


def deal_out(rng, own, number, rows, count, top, most, skew):
    sequence = jax.random.permutation(rng, count)
    packed, common = portions_of(count, rows * top, most, skew, True), portions_of(count, rows * top, most, skew, False)
    places = jnp.arange(count)

    def named(tallies, offset_by):
        used = int((tallies > 0).sum())
        fixed = max(1, used // 4)
        passed = fixed + (places - fixed + offset_by * (used - fixed)) % max(1, count - fixed)
        return jnp.zeros((count,), jnp.int32).at[sequence[jnp.where(places < fixed, places, passed)]].set(jnp.asarray(tallies, jnp.int32))

    tallies = jnp.where(number % 4 == 0, named(packed, number // 4), named(common, number - number // 4 - 1))
    mixed = jax.random.permutation(jax.random.fold_in(own, 3), count)
    source_of, sink = mixed[0:count // 2 * 2:2], mixed[1:count // 2 * 2:2]
    room = jnp.minimum(tallies[source_of] - 1, most - tallies[sink]) // 2
    room = jnp.where((source_of == sequence[0]) | (sink == sequence[0]) | (tallies[sink] == 0), 0, jnp.maximum(room, 0))
    passed = jax.random.randint(jax.random.fold_in(own, 4), (count // 2,), 0, 1 << 20) % (room + 1)
    tallies = tallies.at[source_of].add(-passed).at[sink].add(passed)
    items = jnp.searchsorted(jnp.cumsum(tallies), jnp.arange(rows * top), side="right").astype(jnp.int32)
    table = items.reshape(top, rows).T
    table = table[jax.random.permutation(jax.random.fold_in(own, 1), rows)]
    offset_by = jax.random.randint(jax.random.fold_in(own, 2), (rows, 1), 0, top)
    return jnp.take_along_axis(table, (jnp.arange(top)[None, :] + offset_by) % top, axis=1)


def portions_of(amount, total, limit, lean, full):
    weights = [(1 << 20) // math.isqrt(standing ** lean) + 1 for standing in range(1, amount + 1)]
    largest = limit if full else min(limit, max(-(-total // amount), total * weights[0] // sum(weights)))
    least = 1 if total - largest >= amount - 1 else 0
    holding, spare = [largest] + [least] * (amount - 1), total - largest - least * (amount - 1)
    while spare > 0:
        candidates = [i for i in range(1, amount) if holding[i] < largest] or [i for i in range(1, amount) if holding[i] < limit]
        pool, remaining = sum([weights[i] for i in candidates]), spare
        for i in candidates:
            addition = min(limit - holding[i], max(1, remaining * weights[i] // pool), spare)
            holding[i] = holding[i] + addition
            spare = spare - addition
    return np.array(holding)


def gaussian(rng, shape, scale, reach, cuts=(), held_as=jnp.bfloat16):
    loudness = levels(rng, shape, cuts, -0.22, 0.18) if cuts else 1.0
    entries = jax.random.normal(rng, shape, jnp.float32) * scale * loudness
    return jnp.minimum(jnp.maximum(entries, -reach), reach).astype(held_as)


def setup_inputs(seed: int = 0) -> dict:
    keys = jax.random.split(jax.random.key(seed), 10)
    fluid_vel = gaussian(keys[0], (3, NX, NY, NZ), 1.0, 6.0, ((1, 8), (2, 4)), jnp.float32)
    part_pos = jnp.clip(1.0 * jax.random.uniform(keys[1], (BLOCKS, 3, PER_BLOCK), jnp.float32) ** levels(keys[1], (BLOCKS, 3, PER_BLOCK), ((0, 32),), -0.2, 0.2), 0.0, 1.0)
    part_vel = gaussian(keys[2], (BLOCKS, 3, PER_BLOCK), 1.0, 6.0, ((0, 32),), jnp.float32)
    brick_owner_keys = jax.random.split(jax.random.fold_in(keys[3], 1), BLOCKS // BLK_DEV)
    brick_owner_turns = jax.random.permutation(jax.random.fold_in(keys[3], 3), BLOCKS // BLK_DEV)
    brick_owner = jax.vmap(lambda own, number: deal_out(jax.random.fold_in(keys[3], 2), own, number, BLK_DEV, TILES, 1, CAP, 2))(brick_owner_keys, brick_owner_turns).reshape((BLOCKS, 1))
    brick_local = set_ends(jax.random.randint(keys[4], (BLOCKS,), 0, BRICKS_DEV), jax.random.fold_in(keys[4], 1), 0, BRICKS_DEV - 1).astype(jnp.int32)
    cell_in_brick = set_ends(jax.random.randint(keys[5], (BLOCKS, PER_BLOCK), 0, PER_BLOCK), jax.random.fold_in(keys[5], 1), 0, PER_BLOCK - 1).astype(jnp.int32)
    pair_self = set_ends(jax.random.randint(keys[6], (SUBSTEPS, PAIRS), 0, BLK_DEV), jax.random.fold_in(keys[6], 1), 0, BLK_DEV - 1).astype(jnp.int32)
    pair_other = set_ends(jax.random.randint(keys[7], (SUBSTEPS, PAIRS), 0, BLK_DEV + 2 * HB), jax.random.fold_in(keys[7], 1), 0, (BLK_DEV + 2 * HB) - 1).astype(jnp.int32)
    halo_list = set_ends(jax.random.randint(keys[8], (HALO_ROWS,), 0, BLK_DEV), jax.random.fold_in(keys[8], 1), 0, BLK_DEV - 1).astype(jnp.int32)
    return {"fluid_vel": fluid_vel, "part_pos": part_pos, "part_vel": part_vel, "brick_owner": brick_owner, "brick_local": brick_local, "cell_in_brick": cell_in_brick, "pair_self": pair_self, "pair_other": pair_other, "halo_list": halo_list}


def pair_force(xa, xb):
    dist2 = 0.0025 + (xa[:, 0, :, None] - xb[:, 0, None, :]) ** 2
    dist2 = dist2 + (xa[:, 1, :, None] - xb[:, 1, None, :]) ** 2
    dist2 = dist2 + (xa[:, 2, :, None] - xb[:, 2, None, :]) ** 2
    dist = jnp.sqrt(dist2)
    coef = 10.0 * jnp.maximum(0.25 - dist, 0.0) / dist
    total = lax.optimization_barrier(jnp.sum(coef, axis=2))
    pulled = jnp.einsum('gij,gcj->gci', coef, xb, precision=lax.Precision.HIGHEST)
    return xa * total[:, None, :] - pulled

def to_grid(bricks):
    comps = bricks.shape[2]
    parts = bricks.reshape(N_GX, N_GY, CX // BRICK_X, CY // BRICK_Y, NZ // BRICK_Z, comps, BRICK_X, BRICK_Y, BRICK_Z)
    parts = jnp.transpose(parts, (5, 0, 2, 6, 1, 3, 7, 4, 8))
    return parts.reshape(comps, NX, NY, NZ)

def to_bricks(grid):
    comps = grid.shape[0]
    parts = grid.reshape(comps, N_GX, CX // BRICK_X, BRICK_X, N_GY, CY // BRICK_Y, BRICK_Y, NZ // BRICK_Z, BRICK_Z)
    parts = jnp.transpose(parts, (1, 4, 2, 5, 7, 0, 3, 6, 8))
    return parts.reshape(N_GX * N_GY, BRICKS_DEV, comps, PER_BLOCK)

def reference(fluid_vel, part_pos, part_vel, brick_owner, brick_local, cell_in_brick, pair_self, pair_other, halo_list):
    tiles = N_GX * N_GY
    target = brick_owner[:, 0]
    flat = ((target * BRICKS_DEV + brick_local)[:, None] * PER_BLOCK + cell_in_brick).reshape(-1)
    loads = jnp.concatenate([jnp.ones((BLOCKS, 1, PER_BLOCK), jnp.float32), part_vel], axis=1)
    loads = jnp.transpose(loads, (1, 0, 2)).reshape(4, -1)
    spread = jax.vmap(lambda row: jax.ops.segment_sum(row, flat, num_segments=tiles * BRICKS_DEV * PER_BLOCK))(loads)
    spread = jnp.transpose(spread.reshape(4, tiles, BRICKS_DEV, PER_BLOCK), (1, 2, 0, 3))
    deposit = to_grid(spread)
    count = deposit[0]
    momentum = deposit[1:]
    solid = 0.5 * count
    voids = 1.0 - 0.6 * solid / (1.0 + solid)
    beta = (1.0 - voids) / (voids * voids)
    padded = jnp.pad(fluid_vel, ((0, 0), (1, 1), (1, 1), (1, 1)))
    beside = padded[:, 2:, 1:-1, 1:-1] + padded[:, :-2, 1:-1, 1:-1]
    beside = beside + padded[:, 1:-1, 2:, 1:-1] + padded[:, 1:-1, :-2, 1:-1]
    beside = beside + padded[:, 1:-1, 1:-1, 2:] + padded[:, 1:-1, 1:-1, :-2]
    lap = beside - 6.0 * fluid_vel
    fluid_new = fluid_vel + 0.1 * lap + 0.15 * beta[None] * (momentum - count[None] * fluid_vel)
    table = to_bricks(jnp.concatenate([fluid_new, beta[None]], axis=0))
    mine = table[target, brick_local]
    local_fluid = jnp.take_along_axis(mine, jnp.broadcast_to(cell_in_brick[:, None, :], mine.shape), axis=2)
    flow = local_fluid[:, :3, :]
    drift = 2.0 * local_fluid[:, 3:4, :]
    down = jnp.array([0.0, 0.0, -1.0], jnp.float32)[None, :, None]
    lists = halo_list.reshape(N_GX, N_GY, 2 * HB)
    position = part_pos
    velocity = part_vel
    for step in range(SUBSTEPS):
        grouped = position.reshape(N_GX, N_GY, BLK_DEV, 3, PER_BLOCK)
        index = jnp.broadcast_to(lists[:, :, :, None, None], (N_GX, N_GY, 2 * HB, 3, PER_BLOCK))
        sent = jnp.take_along_axis(grouped, index, axis=2)
        lower = jnp.roll(sent[:, :, HB:], 1, axis=0)
        upper = jnp.roll(sent[:, :, :HB], -1, axis=0)
        extended = jnp.concatenate([grouped, lower, upper], axis=2).reshape(tiles, BLK_DEV + 2 * HB, 3, PER_BLOCK)
        selfs = pair_self[step].reshape(tiles, PAIRS_DEV)
        others = pair_other[step].reshape(tiles, PAIRS_DEV)

        def device_push(item):
            whole, first, second = item
            force = pair_force(whole[first], whole[second])
            return jax.ops.segment_sum(force, first, num_segments=BLK_DEV)
        push = lax.map(device_push, (extended, selfs, others)).reshape(BLOCKS, 3, PER_BLOCK)
        velocity = velocity + 0.1 * (push + drift * (flow - velocity) + down)
        position = position + 0.1 * velocity
    return (fluid_new, position, velocity)
```

```python
import functools
import math

import jax
import jax.numpy as jnp
from jax import lax
from jax.experimental import pallas as pl
from jax.experimental.pallas import tpu as pltpu
from jax.sharding import PartitionSpec as P

SUBSTEPS = 2
BRICK_X = 2
BRICK_Y = 4
BRICK_Z = 16


def padded_2(cells, sides, width, closed):
    for axis, dim in sides:
        count = lax.axis_size(axis)
        ends = count if closed else count - 1
        head = lax.slice_in_dim(cells, 0, width, axis=dim)
        tail = lax.slice_in_dim(cells, cells.shape[dim] - width, cells.shape[dim], axis=dim)
        cells = jnp.concatenate(
            [
                lax.ppermute(tail, axis, [(i, (i + 1) % count) for i in range(ends)]),
                cells,
                lax.ppermute(head, axis, [((i + 1) % count, i) for i in range(ends)]),
            ],
            axis=dim,
        )
    return cells

def split3(x):
    one = x.astype(jnp.bfloat16).astype(jnp.float32)
    rest = x - one
    two = rest.astype(jnp.bfloat16).astype(jnp.float32)
    return one, two, rest - two


def push_kernel(unroll, selfs, others, pos, rims, push, near, far, loads, acc):
    blocks = pos.shape[0]
    pairs = selfs.shape[0]
    size = pos.shape[2]
    eye = (
        lax.broadcasted_iota(jnp.int32, (size, size), 0)
        == lax.broadcasted_iota(jnp.int32, (size, size), 1)
    ).astype(jnp.float32).astype(jnp.bfloat16)
    ones = jnp.ones((1, size), jnp.float32)
    zeros = jnp.zeros((8, size), jnp.float32)

    def side_other(q, raw):
        x = (raw - 0.5) * 0.4
        x1, x2, x3 = split3(x)
        n1, n2, n3 = split3(jnp.sum(x * x, axis=0, keepdims=True))
        rows = jnp.concatenate(
            [x1, n1, x1, n2, x2, n3, x2, ones, x1, ones, x3, ones, zeros], axis=0
        ).astype(jnp.bfloat16)
        turned = lax.dot_general(
            eye, rows, (((1,), (1,)), ((), ())), preferred_element_type=jnp.float32
        )
        far[q] = turned.astype(jnp.bfloat16)
        loads[q] = jnp.concatenate([x1, ones, x2, ones * 0, x3, zeros[:5]], axis=0).astype(
            jnp.bfloat16
        )
        return x1, x2, x3, n1, n2, n3

    def own(q, carry):
        raw = pos[q]
        x1, x2, x3, _, _, _ = side_other(q, raw)
        x = (raw - 0.5) * 0.4
        n1, n2, n3 = split3(jnp.sum(x * x, axis=0, keepdims=True) + 0.0004)
        y1, y2, y3 = -2.0 * x1, -2.0 * x2, -2.0 * x3
        near[q] = jnp.concatenate(
            [y1, ones, y2, ones, y1, ones, y2, n1, y3, n2, y1, n3, zeros], axis=0
        ).astype(jnp.bfloat16)
        acc[q] = jnp.zeros(acc.shape[1:], jnp.float32)
        return carry

    def rim(q, carry):
        side_other(blocks + q, rims[q])
        return carry

    lax.fori_loop(0, blocks, own, 0, unroll=4)
    lax.fori_loop(0, rims.shape[0], rim, 0, unroll=4)

    def some(g, carry):
        sums = []
        for u in range(unroll):
            a = selfs[g * unroll + u]
            b = others[g * unroll + u]
            dist2 = jnp.dot(far[b], near[a], preferred_element_type=jnp.float32)
            w = jnp.maximum(lax.rsqrt(dist2) - 10.0, 0.0)
            high = w.astype(jnp.bfloat16)
            low = (w - high.astype(jnp.float32)).astype(jnp.bfloat16)
            x = loads[b]
            sums.append(
                (
                    a,
                    jnp.dot(
                        jnp.concatenate([x, x], axis=1),
                        jnp.concatenate([high, low], axis=0),
                        preferred_element_type=jnp.float32,
                    ),
                )
            )
        for a, total in sums:
            acc[a] = acc[a] + total
        return carry

    lax.fori_loop(0, pairs // unroll, some, 0)

    def finish(q, carry):
        total = acc[q]
        x = (pos[q] - 0.5) * 0.4
        push[q] = 2.5 * (x * total[3:4] - (total[0:3] + total[4:7] + total[8:11]))
        return carry

    lax.fori_loop(0, blocks, finish, 0, unroll=4)


def contact_push(selfs, others, position, rims):
    blocks, comps, size = position.shape
    ext = blocks + rims.shape[0]
    pairs = selfs.shape[0]
    unroll = math.gcd(pairs, 4)
    vmem = pl.BlockSpec(memory_space=pltpu.VMEM)
    smem = pl.BlockSpec(memory_space=pltpu.SMEM)
    return pl.pallas_call(
        functools.partial(push_kernel, unroll),
        out_shape=jax.ShapeDtypeStruct(position.shape, jnp.float32),
        in_specs=[smem, smem, vmem, vmem],
        out_specs=vmem,
        scratch_shapes=[
            pltpu.VMEM((blocks, 32, size), jnp.bfloat16),
            pltpu.VMEM((ext, size, 32), jnp.bfloat16),
            pltpu.VMEM((ext, 16, size), jnp.bfloat16),
            pltpu.VMEM((blocks, 16, size), jnp.float32),
        ],
        name="contact_push",
    )(selfs, others, position, rims)


def onehot_of(row):
    size = row.shape[1]
    return (lax.broadcasted_iota(jnp.int32, (size, size), 0) == row).astype(
        jnp.float32
    ).astype(jnp.bfloat16)


def deposit_kernel(cells, vel, out):
    size = cells.shape[1]
    ones = jnp.ones((1, size), jnp.float32)
    zeros = jnp.zeros((8, size), jnp.float32)

    def block(q, carry):
        v1, v2, v3 = split3(vel[q])
        rows = jnp.concatenate([ones, v1, zeros[:1], v2, zeros[:1], v3, zeros[:4]], axis=0)
        spots = onehot_of(cells[pl.ds(q, 1), :])
        got = lax.dot_general(
            rows.astype(jnp.bfloat16),
            spots,
            (((1,), (1,)), ((), ())),
            preferred_element_type=jnp.float32,
        )
        out[q] = got[0:4] + got[4:8] + got[8:12]
        return carry

    lax.fori_loop(0, cells.shape[0], block, 0, unroll=4)


def pick_kernel(cells, bricks, out):
    zeros = jnp.zeros((4, cells.shape[1]), jnp.float32)

    def block(q, carry):
        v1, v2, v3 = split3(bricks[q])
        rows = jnp.concatenate([v1, v2, v3, zeros], axis=0)
        spots = onehot_of(cells[pl.ds(q, 1), :])
        got = jnp.dot(rows.astype(jnp.bfloat16), spots, preferred_element_type=jnp.float32)
        out[q] = got[0:4] + got[4:8] + got[8:12]
        return carry

    lax.fori_loop(0, cells.shape[0], block, 0, unroll=4)


def per_block_call(kernel, name, cells, values):
    vmem = pl.BlockSpec(memory_space=pltpu.VMEM)
    blocks, size = cells.shape
    return pl.pallas_call(
        kernel,
        out_shape=jax.ShapeDtypeStruct((blocks, 4, size), jnp.float32),
        in_specs=[vmem, vmem],
        out_specs=vmem,
        name=name,
    )(cells, values)


def grid_bricks(grid):
    comps, sizex, sizey, sizez = grid.shape
    parts = grid.reshape(
        comps, sizex // BRICK_X, BRICK_X, sizey // BRICK_Y, BRICK_Y, sizez // BRICK_Z, BRICK_Z
    )
    parts = jnp.transpose(parts, (1, 3, 5, 0, 2, 4, 6))
    return parts.reshape(-1, comps, BRICK_X * BRICK_Y * BRICK_Z)


def brick_grid(bricks, sizex, sizey, sizez):
    comps = bricks.shape[1]
    parts = bricks.reshape(
        sizex // BRICK_X, sizey // BRICK_Y, sizez // BRICK_Z, comps, BRICK_X, BRICK_Y, BRICK_Z
    )
    parts = jnp.transpose(parts, (3, 0, 4, 1, 5, 2, 6))
    return parts.reshape(comps, sizex, sizey, sizez)


def per_device(
    fluid_vel,
    part_pos,
    part_vel,
    brick_owner,
    brick_local,
    cell_in_brick,
    pair_self,
    pair_other,
    halo_list,
):
    rows_x = lax.axis_size("gx")
    rows_y = lax.axis_size("gy")
    tiles = rows_x * rows_y
    blocks = part_pos.shape[0]
    per_brick = BRICK_X * BRICK_Y * BRICK_Z
    capacity = max(3, 2 * blocks // tiles)
    slots = tiles * capacity
    sizex = fluid_vel.shape[1]
    sizey = fluid_vel.shape[2]
    sizez = fluid_vel.shape[3]
    bricks = sizex // BRICK_X * (sizey // BRICK_Y) * (sizez // BRICK_Z)
    deposit = per_block_call(deposit_kernel, "deposit", cell_in_brick, part_vel)
    target = brick_owner[:, 0]
    chosen = (target[:, None] == jnp.arange(tiles, dtype=jnp.int32)[None, :]).astype(jnp.float32)
    block_iota = jnp.arange(blocks, dtype=jnp.int32)
    earlier = (block_iota[:, None] > block_iota[None, :]).astype(jnp.float32)
    before = jnp.dot(earlier, chosen, precision=lax.Precision.HIGHEST)
    rank = jnp.sum(before * chosen, axis=1).astype(jnp.int32)
    slot = target * capacity + rank
    placing = (jnp.arange(slots, dtype=jnp.int32)[:, None] == slot[None, :]).astype(jnp.float32)
    send_ids = jnp.dot(
        placing, brick_local.astype(jnp.float32), precision=lax.Precision.HIGHEST
    ).astype(jnp.int32)
    send_dep = jnp.dot(
        placing, deposit.reshape(blocks, 4 * per_brick), precision=lax.Precision.HIGHEST
    ).reshape(slots, 4, per_brick)
    got_ids, got_dep = (
        lax.all_to_all(send_ids, ("gx", "gy"), split_axis=0, concat_axis=0, tiled=True),
        lax.all_to_all(send_dep, ("gx", "gy"), split_axis=0, concat_axis=0, tiled=True),
    )
    gathering = (jnp.arange(bricks, dtype=jnp.int32)[:, None] == got_ids[None, :]).astype(
        jnp.float32
    )
    summed = jnp.dot(
        gathering, got_dep.reshape(slots, 4 * per_brick), precision=lax.Precision.HIGHEST
    )
    dep_grid = brick_grid(summed.reshape(bricks, 4, per_brick), sizex, sizey, sizez)
    count = dep_grid[0]
    momentum = dep_grid[1:]
    solid = 0.5 * count
    voids = 1.0 - 0.6 * solid / (1.0 + solid)
    beta = (1.0 - voids) / (voids * voids)
    padded = padded_2(fluid_vel, (("gx", 1), ("gy", 2)), 1, False)
    padded = jnp.pad(padded, ((0, 0), (0, 0), (0, 0), (1, 1)))
    beside = padded[:, 2:, 1:-1, 1:-1] + padded[:, :-2, 1:-1, 1:-1]
    beside = beside + padded[:, 1:-1, 2:, 1:-1] + padded[:, 1:-1, :-2, 1:-1]
    beside = beside + padded[:, 1:-1, 1:-1, 2:] + padded[:, 1:-1, 1:-1, :-2]
    lap = beside - 6.0 * fluid_vel
    fluid_new = fluid_vel + 0.1 * lap + 0.15 * beta[None] * (momentum - count[None] * fluid_vel)
    table = grid_bricks(jnp.concatenate([fluid_new, beta[None]], axis=0))
    answer = table[got_ids]
    back = lax.all_to_all(answer, ("gx", "gy"), split_axis=0, concat_axis=0, tiled=True)
    mine = back[slot]

    local_fluid = per_block_call(pick_kernel, "pick", cell_in_brick, mine)
    flow = local_fluid[:, :3, :]
    drift = 2.0 * local_fluid[:, 3:4, :]
    down = jnp.array([0.0, 0.0, -1.0], jnp.float32)[None, :, None]
    width = halo_list.shape[0] // 2
    position = part_pos
    velocity = part_vel
    for step in range(SUBSTEPS):
        outgoing = position[halo_list]
        rims = padded_2(outgoing, (("gx", 0),), width, True)
        rims = jnp.concatenate([rims[:width], rims[3 * width :]], axis=0)
        push = contact_push(pair_self[step], pair_other[step], position, rims)
        velocity = velocity + 0.1 * (push + drift * (flow - velocity) + down)
        position = position + 0.1 * velocity
    return (fluid_new, position, velocity)


def solution(mesh):
    in_specs = (
        P(None, "gx", "gy", None),
        P(("gx", "gy"), None, None),
        P(("gx", "gy"), None, None),
        P(("gx", "gy"), None),
        P(("gx", "gy")),
        P(("gx", "gy"), None),
        P(None, ("gx", "gy")),
        P(None, ("gx", "gy")),
        P(("gx", "gy")),
    )
    out_specs = (
        P(None, "gx", "gy", None),
        P(("gx", "gy"), None, None),
        P(("gx", "gy"), None, None),
    )
    return jax.shard_map(
        per_device, mesh=mesh, in_specs=in_specs, out_specs=out_specs, check_vma=False
    )
```

```python
import functools
import math

import jax
import jax.numpy as jnp
from jax import lax
from jax.experimental import pallas as pl
from jax.experimental.pallas import tpu as pltpu
from jax.sharding import PartitionSpec as P

SUBSTEPS = 2
BRICK_X = 2
BRICK_Y = 4
BRICK_Z = 16


def padded_2_sides(cells, axis, dim, width, halves):
    count = lax.axis_size(axis)
    ends = count if halves else count - 1
    head = lax.slice_in_dim(cells, 0, width, axis=dim)
    tail = lax.slice_in_dim(cells, cells.shape[dim] - width, cells.shape[dim], axis=dim)
    below = lax.ppermute(tail, axis, [(i, (i + 1) % count) for i in range(ends)])
    above = lax.ppermute(head, axis, [((i + 1) % count, i) for i in range(ends)])
    return below, above


def split3(x):
    one = x.astype(jnp.bfloat16).astype(jnp.float32)
    rest = x - one
    two = rest.astype(jnp.bfloat16).astype(jnp.float32)
    return one, two, rest - two


def push_kernel(unroll, selfs, others, pos, rims, push, near, far, loads, acc):
    blocks = pos.shape[0]
    pairs = selfs.shape[0]
    size = pos.shape[2]
    eye = (
        lax.broadcasted_iota(jnp.int32, (size, size), 0)
        == lax.broadcasted_iota(jnp.int32, (size, size), 1)
    ).astype(jnp.float32).astype(jnp.bfloat16)
    ones = jnp.ones((1, size), jnp.float32)
    zeros = jnp.zeros((8, size), jnp.float32)

    def side_other(q, raw):
        x = (raw - 0.5) * 0.4
        x1, x2, x3 = split3(x)
        n1, n2, n3 = split3(jnp.sum(x * x, axis=0, keepdims=True))
        rows = jnp.concatenate(
            [x1, n1, x1, n2, x2, n3, x2, ones, x1, ones, x3, ones, zeros], axis=0
        ).astype(jnp.bfloat16)
        turned = lax.dot_general(
            eye, rows, (((1,), (1,)), ((), ())), preferred_element_type=jnp.float32
        )
        far[q] = turned.astype(jnp.bfloat16)
        loads[q] = jnp.concatenate([x1, ones, x2, ones * 0, x3, zeros[:5]], axis=0).astype(
            jnp.bfloat16
        )
        return x1, x2, x3, n1, n2, n3

    def own(q, carry):
        raw = pos[q]
        x1, x2, x3, _, _, _ = side_other(q, raw)
        x = (raw - 0.5) * 0.4
        n1, n2, n3 = split3(jnp.sum(x * x, axis=0, keepdims=True) + 0.0004)
        y1, y2, y3 = -2.0 * x1, -2.0 * x2, -2.0 * x3
        near[q] = jnp.concatenate(
            [y1, ones, y2, ones, y1, ones, y2, n1, y3, n2, y1, n3, zeros], axis=0
        ).astype(jnp.bfloat16)
        acc[q] = jnp.zeros(acc.shape[1:], jnp.float32)
        return carry

    def rim(q, carry):
        side_other(blocks + q, rims[q])
        return carry

    lax.fori_loop(0, blocks, own, 0, unroll=16)
    lax.fori_loop(0, rims.shape[0], rim, 0, unroll=8)

    def some(g, carry):
        sums = []
        for u in range(unroll):
            a = selfs[g * unroll + u]
            b = others[g * unroll + u]
            dist2 = jnp.dot(far[b], near[a], preferred_element_type=jnp.float32)
            w = jnp.maximum(lax.rsqrt(dist2) - 10.0, 0.0)
            high = w.astype(jnp.bfloat16)
            low = (w - high.astype(jnp.float32)).astype(jnp.bfloat16)
            x = loads[b]
            sums.append(
                (
                    a,
                    jnp.dot(
                        jnp.concatenate([x, x], axis=1),
                        jnp.concatenate([high, low], axis=0),
                        preferred_element_type=jnp.float32,
                    ),
                )
            )
        for a, total in sums:
            acc[a] = acc[a] + total
        return carry

    lax.fori_loop(0, pairs // unroll, some, 0)

    def finish(q, carry):
        total = acc[q]
        x = (pos[q] - 0.5) * 0.4
        push[q] = 2.5 * (x * total[3:4] - (total[0:3] + total[4:7] + total[8:11]))
        return carry

    lax.fori_loop(0, blocks, finish, 0, unroll=8)


def contact_push(selfs, others, position, rims):
    blocks, comps, size = position.shape
    ext = blocks + rims.shape[0]
    pairs = selfs.shape[0]
    unroll = math.gcd(pairs, 32)
    vmem = pl.BlockSpec(memory_space=pltpu.VMEM)
    smem = pl.BlockSpec(memory_space=pltpu.SMEM)
    return pl.pallas_call(
        functools.partial(push_kernel, unroll),
        out_shape=jax.ShapeDtypeStruct(position.shape, jnp.float32),
        in_specs=[smem, smem, vmem, vmem],
        out_specs=vmem,
        scratch_shapes=[
            pltpu.VMEM((blocks, 32, size), jnp.bfloat16),
            pltpu.VMEM((ext, size, 32), jnp.bfloat16),
            pltpu.VMEM((ext, 16, size), jnp.bfloat16),
            pltpu.VMEM((blocks, 16, size), jnp.float32),
        ],
        cost_estimate=pl.CostEstimate(
            flops=400 * pairs * size * size, bytes_accessed=1 << 22, transcendentals=pairs * size * size
        ),
        name="contact_push",
    )(selfs, others, position, rims)


def onehot_of(row):
    size = row.shape[1]
    return (lax.broadcasted_iota(jnp.int32, (size, size), 0) == row).astype(
        jnp.float32
    ).astype(jnp.bfloat16)


def deposit_kernel(slots, ids, cells, vel, out):
    size = cells.shape[1]
    ones = jnp.ones((1, size), jnp.float32)
    zeros = jnp.zeros((8, size), jnp.float32)
    spot = lax.broadcasted_iota(jnp.int32, (4, size), 1)
    tag = (spot == size - 1) & (lax.broadcasted_iota(jnp.int32, (4, size), 0) == 0)
    empty = jnp.where(tag, -1.0, 0.0)

    def clear(q, carry):
        out[q] = empty
        return carry

    lax.fori_loop(0, out.shape[0], clear, 0, unroll=8)

    def block(q, carry):
        v1, v2, v3 = split3(vel[q])
        rows = jnp.concatenate([ones, v1, zeros[:1], v2, zeros[:1], v3, zeros[:4]], axis=0)
        spots = onehot_of(cells[pl.ds(q, 1), :])
        got = lax.dot_general(
            rows.astype(jnp.bfloat16),
            spots,
            (((1,), (1,)), ((), ())),
            preferred_element_type=jnp.float32,
        )
        total = got[0:4] + got[4:8] + got[8:12]
        out[slots[q]] = jnp.where(tag, ids[q].astype(jnp.float32), total)
        return carry

    lax.fori_loop(0, cells.shape[0], block, 0, unroll=16)


def deposit_blocks(slots, ids, cells, vel, count):
    vmem = pl.BlockSpec(memory_space=pltpu.VMEM)
    smem = pl.BlockSpec(memory_space=pltpu.SMEM)
    return pl.pallas_call(
        deposit_kernel,
        out_shape=jax.ShapeDtypeStruct((count, 4, cells.shape[1]), jnp.float32),
        in_specs=[smem, smem, vmem, vmem],
        out_specs=vmem,
        name="deposit",
    )(slots, ids, cells, vel)


def pick_kernel(slots, cells, bricks, out):
    zeros = jnp.zeros((4, cells.shape[1]), jnp.float32)

    def block(q, carry):
        v1, v2, v3 = split3(bricks[slots[q]])
        rows = jnp.concatenate([v1, v2, v3, zeros], axis=0)
        spots = onehot_of(cells[pl.ds(q, 1), :])
        got = jnp.dot(rows.astype(jnp.bfloat16), spots, preferred_element_type=jnp.float32)
        out[q] = got[0:4] + got[4:8] + got[8:12]
        return carry

    lax.fori_loop(0, cells.shape[0], block, 0, unroll=16)


def pick_cells(slots, cells, bricks):
    vmem = pl.BlockSpec(memory_space=pltpu.VMEM)
    smem = pl.BlockSpec(memory_space=pltpu.SMEM)
    return pl.pallas_call(
        pick_kernel,
        out_shape=jax.ShapeDtypeStruct((cells.shape[0], 4, cells.shape[1]), jnp.float32),
        in_specs=[smem, vmem, vmem],
        out_specs=vmem,
        name="pick",
    )(slots, cells, bricks)


def grid_bricks(grid):
    comps, sizex, sizey, sizez = grid.shape
    parts = grid.reshape(
        comps, sizex // BRICK_X, BRICK_X, sizey // BRICK_Y, BRICK_Y, sizez // BRICK_Z, BRICK_Z
    )
    parts = jnp.transpose(parts, (1, 3, 5, 0, 2, 4, 6))
    return parts.reshape(-1, comps, BRICK_X * BRICK_Y * BRICK_Z)


def brick_grid(bricks, sizex, sizey, sizez):
    comps = bricks.shape[1]
    parts = bricks.reshape(
        sizex // BRICK_X, sizey // BRICK_Y, sizez // BRICK_Z, comps, BRICK_X, BRICK_Y, BRICK_Z
    )
    parts = jnp.transpose(parts, (3, 0, 4, 1, 5, 2, 6))
    return parts.reshape(comps, sizex, sizey, sizez)


def per_device(
    fluid_vel,
    part_pos,
    part_vel,
    brick_owner,
    brick_local,
    cell_in_brick,
    pair_self,
    pair_other,
    halo_list,
):
    rows_x = lax.axis_size("gx")
    rows_y = lax.axis_size("gy")
    tiles = rows_x * rows_y
    blocks = part_pos.shape[0]
    per_brick = BRICK_X * BRICK_Y * BRICK_Z
    capacity = max(3, 2 * blocks // tiles)
    slots = tiles * capacity
    sizex = fluid_vel.shape[1]
    sizey = fluid_vel.shape[2]
    sizez = fluid_vel.shape[3]
    bricks = sizex // BRICK_X * (sizey // BRICK_Y) * (sizez // BRICK_Z)
    width = halo_list.shape[0] // 2
    lower, upper = padded_2_sides(part_pos[halo_list], "gx", 0, width, True)
    rims = jnp.concatenate([lower, upper], axis=0)
    below_x, above_x = padded_2_sides(fluid_vel, "gx", 1, 1, False)
    below_y, above_y = padded_2_sides(fluid_vel, "gy", 2, 1, False)
    target = brick_owner[:, 0]
    chosen = (target[:, None] == jnp.arange(tiles, dtype=jnp.int32)[None, :]).astype(jnp.float32)
    block_iota = jnp.arange(blocks, dtype=jnp.int32)
    earlier = (block_iota[:, None] > block_iota[None, :]).astype(jnp.float32)
    before = jnp.dot(earlier, chosen, precision=lax.Precision.HIGHEST)
    rank = jnp.sum(before * chosen, axis=1).astype(jnp.int32)
    slot = target * capacity + rank
    send_dep = deposit_blocks(slot, brick_local, cell_in_brick, part_vel, slots)
    send_dep, rims, below_x, above_x, below_y, above_y = lax.optimization_barrier(
        (send_dep, rims, below_x, above_x, below_y, above_y)
    )
    got_dep = lax.all_to_all(send_dep, ("gx", "gy"), split_axis=0, concat_axis=0, tiled=True)
    push = contact_push(pair_self[0], pair_other[0], part_pos, rims)
    got_dep, push = lax.optimization_barrier((got_dep, push))
    got_ids = got_dep[:, 0, per_brick - 1].astype(jnp.int32)
    last = jnp.arange(per_brick, dtype=jnp.int32)[None, :] == per_brick - 1
    counts = jnp.where(last, 0.0, got_dep[:, 0, :])
    counts = jnp.where(last, per_brick - jnp.sum(counts, axis=1, keepdims=True), counts)
    got_dep = jnp.concatenate([counts[:, None, :], got_dep[:, 1:, :]], axis=1)
    gathering = (jnp.arange(bricks, dtype=jnp.int32)[:, None] == got_ids[None, :]).astype(
        jnp.float32
    )
    summed = jnp.dot(
        gathering, got_dep.reshape(slots, 4 * per_brick), precision=lax.Precision.HIGHEST
    )
    got_ids = jnp.maximum(got_ids, 0)
    dep_grid = brick_grid(summed.reshape(bricks, 4, per_brick), sizex, sizey, sizez)
    count = dep_grid[0]
    momentum = dep_grid[1:]
    solid = 0.5 * count
    voids = 1.0 - 0.6 * solid / (1.0 + solid)
    beta = (1.0 - voids) / (voids * voids)
    along_x = jnp.concatenate([below_x, fluid_vel, above_x], axis=1)
    along_y = jnp.concatenate([below_y, fluid_vel, above_y], axis=2)
    along_z = jnp.pad(fluid_vel, ((0, 0), (0, 0), (0, 0), (1, 1)))
    beside = along_x[:, 2:] + along_x[:, :-2]
    beside = beside + along_y[:, :, 2:] + along_y[:, :, :-2]
    beside = beside + along_z[:, :, :, 2:] + along_z[:, :, :, :-2]
    lap = beside - 6.0 * fluid_vel
    fluid_new = fluid_vel + 0.1 * lap + 0.15 * beta[None] * (momentum - count[None] * fluid_vel)
    table = grid_bricks(jnp.concatenate([fluid_new, beta[None]], axis=0))
    answer = table[got_ids]
    back = lax.all_to_all(answer, ("gx", "gy"), split_axis=0, concat_axis=0, tiled=True)
    local_fluid = pick_cells(slot, cell_in_brick, back)
    flow = local_fluid[:, :3, :]
    drift = 2.0 * local_fluid[:, 3:4, :]
    down = jnp.array([0.0, 0.0, -1.0], jnp.float32)[None, :, None]
    position = part_pos
    velocity = part_vel
    for step in range(SUBSTEPS):
        if step > 0:
            lower, upper = padded_2_sides(position[halo_list], "gx", 0, width, True)
            rims = jnp.concatenate([lower, upper], axis=0)
            push = contact_push(pair_self[step], pair_other[step], position, rims)
        velocity = velocity + 0.1 * (push + drift * (flow - velocity) + down)
        position = position + 0.1 * velocity
    return (fluid_new, position, velocity)


def solution(mesh):
    in_specs = (
        P(None, "gx", "gy", None),
        P(("gx", "gy"), None, None),
        P(("gx", "gy"), None, None),
        P(("gx", "gy"), None),
        P(("gx", "gy")),
        P(("gx", "gy"), None),
        P(None, ("gx", "gy")),
        P(None, ("gx", "gy")),
        P(("gx", "gy")),
    )
    out_specs = (
        P(None, "gx", "gy", None),
        P(("gx", "gy"), None, None),
        P(("gx", "gy"), None, None),
    )
    return jax.shard_map(
        per_device, mesh=mesh, in_specs=in_specs, out_specs=out_specs, check_vma=False
    )
```

```python
import functools
import math

import jax
import jax.numpy as jnp
from jax import lax
from jax.experimental import pallas as pl
from jax.experimental.pallas import tpu as pltpu
from jax.sharding import PartitionSpec as P

SUBSTEPS = 2
BRICK_X = 2
BRICK_Y = 4
BRICK_Z = 16


def padded_2_sides(cells, axis, dim, width, halves):
    count = lax.axis_size(axis)
    ends = count if halves else count - 1
    head = lax.slice_in_dim(cells, 0, width, axis=dim)
    tail = lax.slice_in_dim(cells, cells.shape[dim] - width, cells.shape[dim], axis=dim)
    below = lax.ppermute(tail, axis, [(i, (i + 1) % count) for i in range(ends)])
    above = lax.ppermute(head, axis, [((i + 1) % count, i) for i in range(ends)])
    return below, above


def split3(x):
    one = x.astype(jnp.bfloat16).astype(jnp.float32)
    rest = x - one
    two = rest.astype(jnp.bfloat16).astype(jnp.float32)
    return one, two, rest - two


def push_kernel(unroll, selfs, others, pos, rims, push, near, far, loads, acc):
    blocks = pos.shape[0]
    pairs = selfs.shape[0]
    size = pos.shape[2]
    eye = (
        lax.broadcasted_iota(jnp.int32, (size, size), 0)
        == lax.broadcasted_iota(jnp.int32, (size, size), 1)
    ).astype(jnp.float32).astype(jnp.bfloat16)
    ones = jnp.ones((1, size), jnp.float32)
    zeros = jnp.zeros((8, size), jnp.float32)

    def side_other(q, raw):
        x = (raw - 0.5) * 0.4
        x1, x2, x3 = split3(x)
        n1, n2, n3 = split3(jnp.sum(x * x, axis=0, keepdims=True))
        rows = jnp.concatenate(
            [x1, n1, x1, n2, x2, n3, x2, ones, x1, ones, x3, ones, zeros], axis=0
        ).astype(jnp.bfloat16)
        turned = lax.dot_general(
            eye, rows, (((1,), (1,)), ((), ())), preferred_element_type=jnp.float32
        )
        far[q] = turned.astype(jnp.bfloat16)
        loads[q] = jnp.concatenate([x1, ones, x2, ones * 0, x3, zeros[:5]], axis=0).astype(
            jnp.bfloat16
        )
        return x1, x2, x3, n1, n2, n3

    def own(q, carry):
        raw = pos[q]
        x1, x2, x3, _, _, _ = side_other(q, raw)
        x = (raw - 0.5) * 0.4
        n1, n2, n3 = split3(jnp.sum(x * x, axis=0, keepdims=True) + 0.0004)
        y1, y2, y3 = -2.0 * x1, -2.0 * x2, -2.0 * x3
        near[q] = jnp.concatenate(
            [y1, ones, y2, ones, y1, ones, y2, n1, y3, n2, y1, n3, zeros], axis=0
        ).astype(jnp.bfloat16)
        acc[q] = jnp.zeros(acc.shape[1:], jnp.float32)
        return carry

    def rim(q, carry):
        side_other(blocks + q, rims[q])
        return carry

    lax.fori_loop(0, blocks, own, 0, unroll=16)
    lax.fori_loop(0, rims.shape[0], rim, 0, unroll=8)

    def some(g, carry):
        sums = []
        for u in range(unroll):
            a = selfs[g * unroll + u]
            b = others[g * unroll + u]
            dist2 = jnp.dot(far[b], near[a], preferred_element_type=jnp.float32)
            w = jnp.maximum(lax.rsqrt(dist2) - 10.0, 0.0)
            high = w.astype(jnp.bfloat16)
            low = (w - high.astype(jnp.float32)).astype(jnp.bfloat16)
            x = loads[b]
            sums.append(
                (
                    a,
                    jnp.dot(
                        jnp.concatenate([x, x], axis=1),
                        jnp.concatenate([high, low], axis=0),
                        preferred_element_type=jnp.float32,
                    ),
                )
            )
        for a, total in sums:
            acc[a] = acc[a] + total
        return carry

    lax.fori_loop(0, pairs // unroll, some, 0)

    def finish(q, carry):
        total = acc[q]
        x = (pos[q] - 0.5) * 0.4
        push[q] = 2.5 * (x * total[3:4] - (total[0:3] + total[4:7] + total[8:11]))
        return carry

    lax.fori_loop(0, blocks, finish, 0, unroll=8)


def contact_push(selfs, others, position, rims):
    blocks, comps, size = position.shape
    ext = blocks + rims.shape[0]
    pairs = selfs.shape[0]
    unroll = math.gcd(pairs, 32)
    vmem = pl.BlockSpec(memory_space=pltpu.VMEM)
    smem = pl.BlockSpec(memory_space=pltpu.SMEM)
    return pl.pallas_call(
        functools.partial(push_kernel, unroll),
        out_shape=jax.ShapeDtypeStruct(position.shape, jnp.float32),
        in_specs=[smem, smem, vmem, vmem],
        out_specs=vmem,
        scratch_shapes=[
            pltpu.VMEM((blocks, 32, size), jnp.bfloat16),
            pltpu.VMEM((ext, size, 32), jnp.bfloat16),
            pltpu.VMEM((ext, 16, size), jnp.bfloat16),
            pltpu.VMEM((blocks, 16, size), jnp.float32),
        ],
        cost_estimate=pl.CostEstimate(
            flops=400 * pairs * size * size, bytes_accessed=1 << 22, transcendentals=pairs * size * size
        ),
        name="contact_push",
    )(selfs, others, position, rims)


def onehot_of(row):
    size = row.shape[1]
    return (lax.broadcasted_iota(jnp.int32, (size, size), 0) == row).astype(
        jnp.float32
    ).astype(jnp.bfloat16)


def deposit_kernel(slots, ids, cells, vel, out):
    size = cells.shape[1]
    ones = jnp.ones((1, size), jnp.float32)
    zeros = jnp.zeros((8, size), jnp.float32)
    spot = lax.broadcasted_iota(jnp.int32, (4, size), 1)
    tag = (spot == size - 1) & (lax.broadcasted_iota(jnp.int32, (4, size), 0) == 0)
    empty = jnp.where(tag, -1.0, 0.0)

    def clear(q, carry):
        out[q] = empty
        return carry

    lax.fori_loop(0, out.shape[0], clear, 0, unroll=8)

    def block(q, carry):
        v1, v2, v3 = split3(vel[q])
        rows = jnp.concatenate([ones, v1, zeros[:1], v2, zeros[:1], v3, zeros[:4]], axis=0)
        spots = onehot_of(cells[pl.ds(q, 1), :])
        got = lax.dot_general(
            rows.astype(jnp.bfloat16),
            spots,
            (((1,), (1,)), ((), ())),
            preferred_element_type=jnp.float32,
        )
        total = got[0:4] + got[4:8] + got[8:12]
        out[slots[q]] = jnp.where(tag, ids[q].astype(jnp.float32), total)
        return carry

    lax.fori_loop(0, cells.shape[0], block, 0, unroll=16)


def deposit_blocks(slots, ids, cells, vel, count):
    vmem = pl.BlockSpec(memory_space=pltpu.VMEM)
    smem = pl.BlockSpec(memory_space=pltpu.SMEM)
    return pl.pallas_call(
        deposit_kernel,
        out_shape=jax.ShapeDtypeStruct((count, 4, cells.shape[1]), jnp.float32),
        in_specs=[smem, smem, vmem, vmem],
        out_specs=vmem,
        name="deposit",
    )(slots, ids, cells, vel)


def pick_kernel(slots, cells, bricks, out):
    zeros = jnp.zeros((4, cells.shape[1]), jnp.float32)

    def block(q, carry):
        v1, v2, v3 = split3(bricks[slots[q]])
        rows = jnp.concatenate([v1, v2, v3, zeros], axis=0)
        spots = onehot_of(cells[pl.ds(q, 1), :])
        got = jnp.dot(rows.astype(jnp.bfloat16), spots, preferred_element_type=jnp.float32)
        out[q] = got[0:4] + got[4:8] + got[8:12]
        return carry

    lax.fori_loop(0, cells.shape[0], block, 0, unroll=16)


def pick_cells(slots, cells, bricks):
    vmem = pl.BlockSpec(memory_space=pltpu.VMEM)
    smem = pl.BlockSpec(memory_space=pltpu.SMEM)
    return pl.pallas_call(
        pick_kernel,
        out_shape=jax.ShapeDtypeStruct((cells.shape[0], 4, cells.shape[1]), jnp.float32),
        in_specs=[smem, vmem, vmem],
        out_specs=vmem,
        name="pick",
    )(slots, cells, bricks)


def same(left, right):
    return (left == right).astype(jnp.float32).astype(jnp.bfloat16)


def parts_of(x, axis):
    return jnp.concatenate([part.astype(jnp.bfloat16) for part in split3(x)], axis=axis)


def grid_kernel(got, fluid, base, fresh, answer, spread, rows, table):
    slots, _, size = got.shape
    _, sizex, sizey, sizez = fluid.shape
    along_y, along_z = sizey // BRICK_Y, sizez // BRICK_Z
    groups = sizex // BRICK_X * along_y
    bricks = groups * along_z
    lines = BRICK_X * BRICK_Y

    def iota(shape, dim):
        return lax.broadcasted_iota(jnp.int32, shape, dim)

    first = got[:, 0, :]
    last = iota((slots, size), 1) == size - 1
    named = same(first[:, size - 1 : size], iota((slots, bricks), 1).astype(jnp.float32))
    counts = jnp.where(last, 0.0, first)
    counts = jnp.where(last, size - jnp.sum(counts, axis=1, keepdims=True), counts)
    loads = [counts.astype(jnp.bfloat16)] + [parts_of(got[:, 1 + m, :], 1) for m in range(3)]
    summed = lax.dot_general(
        named,
        jnp.concatenate(loads, axis=1),
        (((0,), (0,)), ((), ())),
        preferred_element_type=jnp.float32,
    )
    count = summed[:, :size]
    solid = 0.5 * count
    voids = 1.0 - 0.6 * solid / (1.0 + solid)
    beta = (1.0 - voids) / (voids * voids)
    scale = 0.15 * beta
    table[3] = beta
    terms = [scale * count]
    for m in range(3):
        at = size * (1 + 3 * m)
        momentum = summed[:, at : at + size] + summed[:, at + size : at + 2 * size]
        terms.append(scale * (momentum + summed[:, at + 2 * size : at + 3 * size]))
    keep = iota((bricks, sizez), 0) % along_z == iota((bricks, sizez), 1) // BRICK_Z
    where_z = iota((size, sizez), 1) % BRICK_Z
    for k in range(4):
        term = parts_of(terms[k], 1)
        for r in range(lines):
            choice = same(iota((size, sizez), 0), r * BRICK_Z + where_z)
            wide = jnp.dot(
                term, jnp.concatenate([choice] * 3, axis=0), preferred_element_type=jnp.float32
            )
            wide = jnp.where(keep, wide, 0.0).reshape(groups, along_z, sizez)
            spread[k, :, r, :] = jnp.sum(wide, axis=1)
    for m in range(3):
        for g in range(groups):
            for dx in range(BRICK_X):
                x = g // along_y * BRICK_X + dx
                y = pl.ds(g % along_y * BRICK_Y, BRICK_Y)
                line = pl.ds(dx * BRICK_Y, BRICK_Y)
                held = fluid[m, x, y, :]
                value = base[m, x, y, :] + (spread[1 + m, g, line, :] - spread[0, g, line, :] * held)
                fresh[m, x, y, :] = value
                rows[m, g, line, :] = value
    for m in range(3):
        every = parts_of(rows[m].reshape(groups * lines, sizez), 1)
        mine = (
            iota((groups * lines, size), 0) % lines == iota((groups * lines, size), 1) // BRICK_Z
        )
        for z in range(along_z):
            choice = same(
                iota((sizez, size), 0), z * BRICK_Z + iota((sizez, size), 1) % BRICK_Z
            )
            narrow = jnp.dot(
                every, jnp.concatenate([choice] * 3, axis=0), preferred_element_type=jnp.float32
            )
            narrow = jnp.where(mine, narrow, 0.0).reshape(groups, lines, size)
            table[m, pl.ds(z, groups, stride=along_z), :] = jnp.sum(narrow, axis=1)
    for k in range(4):
        answer[:, k, :] = jnp.dot(
            jnp.concatenate([named] * 3, axis=1),
            parts_of(table[k], 0),
            preferred_element_type=jnp.float32,
        )


def grid_step(got, fluid, base):
    vmem = pl.BlockSpec(memory_space=pltpu.VMEM)
    _, sizex, sizey, sizez = fluid.shape
    groups = sizex // BRICK_X * (sizey // BRICK_Y)
    lines = BRICK_X * BRICK_Y
    bricks = groups * (sizez // BRICK_Z)
    return pl.pallas_call(
        grid_kernel,
        out_shape=(
            jax.ShapeDtypeStruct(fluid.shape, jnp.float32),
            jax.ShapeDtypeStruct(got.shape, jnp.float32),
        ),
        in_specs=[vmem] * 3,
        out_specs=(vmem, vmem),
        scratch_shapes=[
            pltpu.VMEM((4, groups, lines, sizez), jnp.float32),
            pltpu.VMEM((3, groups, lines, sizez), jnp.float32),
            pltpu.VMEM((4, bricks, got.shape[2]), jnp.float32),
        ],
        name="grid_step",
    )(got, fluid, base)


def per_device(
    fluid_vel,
    part_pos,
    part_vel,
    brick_owner,
    brick_local,
    cell_in_brick,
    pair_self,
    pair_other,
    halo_list,
):
    rows_x = lax.axis_size("gx")
    rows_y = lax.axis_size("gy")
    tiles = rows_x * rows_y
    blocks = part_pos.shape[0]
    capacity = max(3, 2 * blocks // tiles)
    slots = tiles * capacity
    width = halo_list.shape[0] // 2
    lower, upper = padded_2_sides(part_pos[halo_list], "gx", 0, width, True)
    rims = jnp.concatenate([lower, upper], axis=0)
    below_x, above_x = padded_2_sides(fluid_vel, "gx", 1, 1, False)
    below_y, above_y = padded_2_sides(fluid_vel, "gy", 2, 1, False)
    target = brick_owner[:, 0]
    chosen = (target[:, None] == jnp.arange(tiles, dtype=jnp.int32)[None, :]).astype(jnp.float32)
    block_iota = jnp.arange(blocks, dtype=jnp.int32)
    earlier = (block_iota[:, None] > block_iota[None, :]).astype(jnp.float32)
    before = jnp.dot(earlier, chosen, precision=lax.Precision.HIGHEST)
    rank = jnp.sum(before * chosen, axis=1).astype(jnp.int32)
    slot = target * capacity + rank
    send_dep = deposit_blocks(slot, brick_local, cell_in_brick, part_vel, slots)
    send_dep, rims, below_x, above_x, below_y, above_y = lax.optimization_barrier(
        (send_dep, rims, below_x, above_x, below_y, above_y)
    )
    got_dep = lax.all_to_all(send_dep, ("gx", "gy"), split_axis=0, concat_axis=0, tiled=True)
    push = contact_push(pair_self[0], pair_other[0], part_pos, rims)
    along_x = jnp.concatenate([below_x, fluid_vel, above_x], axis=1)
    along_y = jnp.concatenate([below_y, fluid_vel, above_y], axis=2)
    along_z = jnp.pad(fluid_vel, ((0, 0), (0, 0), (0, 0), (1, 1)))
    beside = along_x[:, 2:] + along_x[:, :-2]
    beside = beside + along_y[:, :, 2:] + along_y[:, :, :-2]
    beside = beside + along_z[:, :, :, 2:] + along_z[:, :, :, :-2]
    base = fluid_vel + 0.1 * (beside - 6.0 * fluid_vel)
    got_dep, push, base = lax.optimization_barrier((got_dep, push, base))
    fluid_new, answer = grid_step(got_dep, fluid_vel, base)
    back = lax.all_to_all(answer, ("gx", "gy"), split_axis=0, concat_axis=0, tiled=True)
    local_fluid = pick_cells(slot, cell_in_brick, back)
    flow = local_fluid[:, :3, :]
    drift = 2.0 * local_fluid[:, 3:4, :]
    down = jnp.array([0.0, 0.0, -1.0], jnp.float32)[None, :, None]
    position = part_pos
    velocity = part_vel
    for step in range(SUBSTEPS):
        if step > 0:
            lower, upper = padded_2_sides(position[halo_list], "gx", 0, width, True)
            rims = jnp.concatenate([lower, upper], axis=0)
            push = contact_push(pair_self[step], pair_other[step], position, rims)
        velocity = velocity + 0.1 * (push + drift * (flow - velocity) + down)
        position = position + 0.1 * velocity
    return (fluid_new, position, velocity)


def solution(mesh):
    in_specs = (
        P(None, "gx", "gy", None),
        P(("gx", "gy"), None, None),
        P(("gx", "gy"), None, None),
        P(("gx", "gy"), None),
        P(("gx", "gy")),
        P(("gx", "gy"), None),
        P(None, ("gx", "gy")),
        P(None, ("gx", "gy")),
        P(("gx", "gy")),
    )
    out_specs = (
        P(None, "gx", "gy", None),
        P(("gx", "gy"), None, None),
        P(("gx", "gy"), None, None),
    )
    return jax.shard_map(
        per_device, mesh=mesh, in_specs=in_specs, out_specs=out_specs, check_vma=False
    )
```

```python
import functools
import math

import jax
import jax.numpy as jnp
from jax import lax
from jax.experimental import pallas as pl
from jax.experimental.pallas import tpu as pltpu
from jax.sharding import PartitionSpec as P

SUBSTEPS = 2
BRICK_X = 2
BRICK_Y = 4
BRICK_Z = 16


def padded_2_sides(cells, axis, dim, width, halves):
    count = lax.axis_size(axis)
    ends = count if halves else count - 1
    head = lax.slice_in_dim(cells, 0, width, axis=dim)
    tail = lax.slice_in_dim(cells, cells.shape[dim] - width, cells.shape[dim], axis=dim)
    below = lax.ppermute(tail, axis, [(i, (i + 1) % count) for i in range(ends)])
    above = lax.ppermute(head, axis, [((i + 1) % count, i) for i in range(ends)])
    return below, above


def split3(x):
    one = x.astype(jnp.bfloat16).astype(jnp.float32)
    rest = x - one
    two = rest.astype(jnp.bfloat16).astype(jnp.float32)
    return one, two, rest - two


def push_kernel(unroll, selfs, others, pos, rims, push, near, far, loads, acc):
    blocks = pos.shape[0]
    pairs = selfs.shape[0]
    size = pos.shape[2]
    eye = (
        lax.broadcasted_iota(jnp.int32, (size, size), 0)
        == lax.broadcasted_iota(jnp.int32, (size, size), 1)
    ).astype(jnp.float32).astype(jnp.bfloat16)
    ones = jnp.ones((1, size), jnp.float32)
    zeros = jnp.zeros((8, size), jnp.float32)

    def side_other(q, raw):
        x = (raw - 0.5) * 0.4
        x1, x2, x3 = split3(x)
        n1, n2, n3 = split3(jnp.sum(x * x, axis=0, keepdims=True))
        rows = jnp.concatenate(
            [x1, n1, x1, n2, x2, n3, x2, ones, x1, ones, x3, ones, zeros], axis=0
        ).astype(jnp.bfloat16)
        turned = lax.dot_general(
            eye, rows, (((1,), (1,)), ((), ())), preferred_element_type=jnp.float32
        )
        far[q] = turned.astype(jnp.bfloat16)
        loads[q] = jnp.concatenate([x1, ones, x2, ones * 0, x3, zeros[:5]], axis=0).astype(
            jnp.bfloat16
        )
        return x1, x2, x3, n1, n2, n3

    def own(q, carry):
        raw = pos[q]
        x1, x2, x3, _, _, _ = side_other(q, raw)
        x = (raw - 0.5) * 0.4
        n1, n2, n3 = split3(jnp.sum(x * x, axis=0, keepdims=True) + 0.0004)
        y1, y2, y3 = -2.0 * x1, -2.0 * x2, -2.0 * x3
        near[q] = jnp.concatenate(
            [y1, ones, y2, ones, y1, ones, y2, n1, y3, n2, y1, n3, zeros], axis=0
        ).astype(jnp.bfloat16)
        acc[q] = jnp.zeros(acc.shape[1:], jnp.float32)
        return carry

    def rim(q, carry):
        side_other(blocks + q, rims[q])
        return carry

    lax.fori_loop(0, blocks, own, 0, unroll=16)
    lax.fori_loop(0, rims.shape[0], rim, 0, unroll=8)

    def some(g, carry):
        sums = []
        for u in range(unroll):
            a = selfs[g * unroll + u]
            b = others[g * unroll + u]
            dist2 = jnp.dot(far[b], near[a], preferred_element_type=jnp.float32)
            w = jnp.maximum(lax.rsqrt(dist2) - 10.0, 0.0)
            high = w.astype(jnp.bfloat16)
            low = (w - high.astype(jnp.float32)).astype(jnp.bfloat16)
            x = loads[b]
            sums.append(
                (
                    a,
                    jnp.dot(
                        jnp.concatenate([x, x], axis=1),
                        jnp.concatenate([high, low], axis=0),
                        preferred_element_type=jnp.float32,
                    ),
                )
            )
        for a, total in sums:
            acc[a] = acc[a] + total
        return carry

    lax.fori_loop(0, pairs // unroll, some, 0)

    def finish(q, carry):
        total = acc[q]
        x = (pos[q] - 0.5) * 0.4
        push[q] = 2.5 * (x * total[3:4] - (total[0:3] + total[4:7] + total[8:11]))
        return carry

    lax.fori_loop(0, blocks, finish, 0, unroll=8)


def contact_push(selfs, others, position, rims):
    blocks, comps, size = position.shape
    ext = blocks + rims.shape[0]
    pairs = selfs.shape[0]
    unroll = math.gcd(pairs, 32)
    vmem = pl.BlockSpec(memory_space=pltpu.VMEM)
    smem = pl.BlockSpec(memory_space=pltpu.SMEM)
    return pl.pallas_call(
        functools.partial(push_kernel, unroll),
        out_shape=jax.ShapeDtypeStruct(position.shape, jnp.float32),
        in_specs=[smem, smem, vmem, vmem],
        out_specs=vmem,
        scratch_shapes=[
            pltpu.VMEM((blocks, 32, size), jnp.bfloat16),
            pltpu.VMEM((ext, size, 32), jnp.bfloat16),
            pltpu.VMEM((ext, 16, size), jnp.bfloat16),
            pltpu.VMEM((blocks, 16, size), jnp.float32),
        ],
        cost_estimate=pl.CostEstimate(
            flops=400 * pairs * size * size, bytes_accessed=1 << 22, transcendentals=pairs * size * size
        ),
        name="contact_push",
    )(selfs, others, position, rims)


def onehot_of(row):
    size = row.shape[1]
    return (lax.broadcasted_iota(jnp.int32, (size, size), 0) == row).astype(
        jnp.float32
    ).astype(jnp.bfloat16)


def deposit_kernel(slots, ids, cells, vel, out):
    size = cells.shape[1]
    ones = jnp.ones((1, size), jnp.float32)
    zeros = jnp.zeros((8, size), jnp.float32)
    spot = lax.broadcasted_iota(jnp.int32, (4, size), 1)
    tag = (spot == size - 1) & (lax.broadcasted_iota(jnp.int32, (4, size), 0) == 0)
    empty = jnp.where(tag, -1.0, 0.0)

    def clear(q, carry):
        out[q] = empty
        return carry

    lax.fori_loop(0, out.shape[0], clear, 0, unroll=8)

    def block(q, carry):
        v1, v2, v3 = split3(vel[q])
        rows = jnp.concatenate([ones, v1, zeros[:1], v2, zeros[:1], v3, zeros[:4]], axis=0)
        spots = onehot_of(cells[pl.ds(q, 1), :])
        got = lax.dot_general(
            rows.astype(jnp.bfloat16),
            spots,
            (((1,), (1,)), ((), ())),
            preferred_element_type=jnp.float32,
        )
        total = got[0:4] + got[4:8] + got[8:12]
        out[slots[q]] = jnp.where(tag, ids[q].astype(jnp.float32), total)
        return carry

    lax.fori_loop(0, cells.shape[0], block, 0, unroll=16)


def deposit_blocks(slots, ids, cells, vel, count):
    vmem = pl.BlockSpec(memory_space=pltpu.VMEM)
    smem = pl.BlockSpec(memory_space=pltpu.SMEM)
    return pl.pallas_call(
        deposit_kernel,
        out_shape=jax.ShapeDtypeStruct((count, 4, cells.shape[1]), jnp.float32),
        in_specs=[smem, smem, vmem, vmem],
        out_specs=vmem,
        name="deposit",
    )(slots, ids, cells, vel)


def pick_kernel(slots, cells, bricks, out):
    zeros = jnp.zeros((4, cells.shape[1]), jnp.float32)

    def block(q, carry):
        v1, v2, v3 = split3(bricks[slots[q]])
        rows = jnp.concatenate([v1, v2, v3, zeros], axis=0)
        spots = onehot_of(cells[pl.ds(q, 1), :])
        got = jnp.dot(rows.astype(jnp.bfloat16), spots, preferred_element_type=jnp.float32)
        out[q] = got[0:4] + got[4:8] + got[8:12]
        return carry

    lax.fori_loop(0, cells.shape[0], block, 0, unroll=16)


def pick_cells(slots, cells, bricks):
    vmem = pl.BlockSpec(memory_space=pltpu.VMEM)
    smem = pl.BlockSpec(memory_space=pltpu.SMEM)
    return pl.pallas_call(
        pick_kernel,
        out_shape=jax.ShapeDtypeStruct((cells.shape[0], 4, cells.shape[1]), jnp.float32),
        in_specs=[smem, vmem, vmem],
        out_specs=vmem,
        name="pick",
    )(slots, cells, bricks)


def same(left, right):
    return (left == right).astype(jnp.float32).astype(jnp.bfloat16)


def parts_of(x, axis):
    return jnp.concatenate([part.astype(jnp.bfloat16) for part in split3(x)], axis=axis)


def grid_kernel(got, fluid, base, fresh, answer, spread, rows, table):
    slots, _, size = got.shape
    _, sizex, sizey, sizez = fluid.shape
    along_y, along_z = sizey // BRICK_Y, sizez // BRICK_Z
    groups = sizex // BRICK_X * along_y
    bricks = groups * along_z
    lines = BRICK_X * BRICK_Y

    def iota(shape, dim):
        return lax.broadcasted_iota(jnp.int32, shape, dim)

    first = got[:, 0, :]
    last = iota((slots, size), 1) == size - 1
    named = same(first[:, size - 1 : size], iota((slots, bricks), 1).astype(jnp.float32))
    counts = jnp.where(last, 0.0, first)
    counts = jnp.where(last, size - jnp.sum(counts, axis=1, keepdims=True), counts)
    loads = [counts.astype(jnp.bfloat16)] + [parts_of(got[:, 1 + m, :], 1) for m in range(3)]
    summed = lax.dot_general(
        named,
        jnp.concatenate(loads, axis=1),
        (((0,), (0,)), ((), ())),
        preferred_element_type=jnp.float32,
    )
    count = summed[:, :size]
    solid = 0.5 * count
    voids = 1.0 - 0.6 * solid / (1.0 + solid)
    beta = (1.0 - voids) / (voids * voids)
    scale = 0.15 * beta
    table[3] = beta
    terms = [scale * count]
    for m in range(3):
        at = size * (1 + 3 * m)
        momentum = summed[:, at : at + size] + summed[:, at + size : at + 2 * size]
        terms.append(scale * (momentum + summed[:, at + 2 * size : at + 3 * size]))
    keep = iota((bricks, sizez), 0) % along_z == iota((bricks, sizez), 1) // BRICK_Z
    where_z = iota((size, sizez), 1) % BRICK_Z
    for k in range(4):
        term = parts_of(terms[k], 1)
        for r in range(lines):
            choice = same(iota((size, sizez), 0), r * BRICK_Z + where_z)
            wide = jnp.dot(
                term, jnp.concatenate([choice] * 3, axis=0), preferred_element_type=jnp.float32
            )
            wide = jnp.where(keep, wide, 0.0).reshape(groups, along_z, sizez)
            spread[k, :, r, :] = jnp.sum(wide, axis=1)
    for m in range(3):
        for g in range(groups):
            for dx in range(BRICK_X):
                x = g // along_y * BRICK_X + dx
                y = pl.ds(g % along_y * BRICK_Y, BRICK_Y)
                line = pl.ds(dx * BRICK_Y, BRICK_Y)
                held = fluid[m, x, y, :]
                value = base[m, x, y, :] + (spread[1 + m, g, line, :] - spread[0, g, line, :] * held)
                fresh[m, x, y, :] = value
                rows[m, g, line, :] = value
    for m in range(3):
        every = parts_of(rows[m].reshape(groups * lines, sizez), 1)
        mine = (
            iota((groups * lines, size), 0) % lines == iota((groups * lines, size), 1) // BRICK_Z
        )
        for z in range(along_z):
            choice = same(
                iota((sizez, size), 0), z * BRICK_Z + iota((sizez, size), 1) % BRICK_Z
            )
            narrow = jnp.dot(
                every, jnp.concatenate([choice] * 3, axis=0), preferred_element_type=jnp.float32
            )
            narrow = jnp.where(mine, narrow, 0.0).reshape(groups, lines, size)
            table[m, pl.ds(z, groups, stride=along_z), :] = jnp.sum(narrow, axis=1)
    for k in range(4):
        answer[:, k, :] = jnp.dot(
            jnp.concatenate([named] * 3, axis=1),
            parts_of(table[k], 0),
            preferred_element_type=jnp.float32,
        )


def grid_step(got, fluid, base):
    vmem = pl.BlockSpec(memory_space=pltpu.VMEM)
    _, sizex, sizey, sizez = fluid.shape
    groups = sizex // BRICK_X * (sizey // BRICK_Y)
    lines = BRICK_X * BRICK_Y
    bricks = groups * (sizez // BRICK_Z)
    return pl.pallas_call(
        grid_kernel,
        out_shape=(
            jax.ShapeDtypeStruct(fluid.shape, jnp.float32),
            jax.ShapeDtypeStruct(got.shape, jnp.float32),
        ),
        in_specs=[vmem] * 3,
        out_specs=(vmem, vmem),
        scratch_shapes=[
            pltpu.VMEM((4, groups, lines, sizez), jnp.float32),
            pltpu.VMEM((3, groups, lines, sizez), jnp.float32),
            pltpu.VMEM((4, bricks, got.shape[2]), jnp.float32),
        ],
        name="grid_step",
    )(got, fluid, base)


def per_device(
    fluid_vel,
    part_pos,
    part_vel,
    brick_owner,
    brick_local,
    cell_in_brick,
    pair_self,
    pair_other,
    halo_list,
):
    rows_x = lax.axis_size("gx")
    rows_y = lax.axis_size("gy")
    tiles = rows_x * rows_y
    blocks = part_pos.shape[0]
    capacity = max(3, 2 * blocks // tiles)
    slots = tiles * capacity
    width = halo_list.shape[0] // 2
    target = brick_owner[:, 0]
    chosen = (target[:, None] == jnp.arange(tiles, dtype=jnp.int32)[None, :]).astype(jnp.float32)
    block_iota = jnp.arange(blocks, dtype=jnp.int32)
    earlier = (block_iota[:, None] > block_iota[None, :]).astype(jnp.float32)
    before = jnp.dot(earlier, chosen, precision=lax.Precision.HIGHEST)
    rank = jnp.sum(before * chosen, axis=1).astype(jnp.int32)
    slot = target * capacity + rank
    send_dep = deposit_blocks(slot, brick_local, cell_in_brick, part_vel, slots)
    edge_blocks = part_pos[halo_list]
    send_dep, edge_blocks, fluid = lax.optimization_barrier((send_dep, edge_blocks, fluid_vel))
    got_dep = lax.all_to_all(send_dep, ("gx", "gy"), split_axis=0, concat_axis=0, tiled=True)
    lower, upper = padded_2_sides(edge_blocks, "gx", 0, width, True)
    rims = jnp.concatenate([lower, upper], axis=0)
    below_x, above_x = padded_2_sides(fluid, "gx", 1, 1, False)
    below_y, above_y = padded_2_sides(fluid, "gy", 2, 1, False)
    along_x = jnp.concatenate([below_x, fluid_vel, above_x], axis=1)
    along_y = jnp.concatenate([below_y, fluid_vel, above_y], axis=2)
    along_z = jnp.pad(fluid_vel, ((0, 0), (0, 0), (0, 0), (1, 1)))
    beside = along_x[:, 2:] + along_x[:, :-2]
    beside = beside + along_y[:, :, 2:] + along_y[:, :, :-2]
    beside = beside + along_z[:, :, :, 2:] + along_z[:, :, :, :-2]
    base = fluid_vel + 0.1 * (beside - 6.0 * fluid_vel)
    got_dep, base, rims = lax.optimization_barrier((got_dep, base, rims))
    fluid_new, answer = grid_step(got_dep, fluid_vel, base)
    answer, rims = lax.optimization_barrier((answer, rims))
    back = lax.all_to_all(answer, ("gx", "gy"), split_axis=0, concat_axis=0, tiled=True)
    push = contact_push(pair_self[0], pair_other[0], part_pos, rims)
    back, push = lax.optimization_barrier((back, push))
    local_fluid = pick_cells(slot, cell_in_brick, back)
    flow = local_fluid[:, :3, :]
    drift = 2.0 * local_fluid[:, 3:4, :]
    down = jnp.array([0.0, 0.0, -1.0], jnp.float32)[None, :, None]
    position = part_pos
    velocity = part_vel
    for step in range(SUBSTEPS):
        if step > 0:
            lower, upper = padded_2_sides(position[halo_list], "gx", 0, width, True)
            rims = jnp.concatenate([lower, upper], axis=0)
            push = contact_push(pair_self[step], pair_other[step], position, rims)
        velocity = velocity + 0.1 * (push + drift * (flow - velocity) + down)
        position = position + 0.1 * velocity
    return (fluid_new, position, velocity)


def solution(mesh):
    in_specs = (
        P(None, "gx", "gy", None),
        P(("gx", "gy"), None, None),
        P(("gx", "gy"), None, None),
        P(("gx", "gy"), None),
        P(("gx", "gy")),
        P(("gx", "gy"), None),
        P(None, ("gx", "gy")),
        P(None, ("gx", "gy")),
        P(("gx", "gy")),
    )
    out_specs = (
        P(None, "gx", "gy", None),
        P(("gx", "gy"), None, None),
        P(("gx", "gy"), None, None),
    )
    return jax.shard_map(
        per_device, mesh=mesh, in_specs=in_specs, out_specs=out_specs, check_vma=False
    )
```
